1024 devices in a mesh: expert: 16 (over y, x), fsdp: 64 (over z, core).
Axes of the slice: x: 4, y: 4, z: 32, core: 2. Of those that a mesh axis runs over, the one named last changes fastest.
Arguments:
- out_grad: bfloat16 [262144, 2048], P(('expert', 'fsdp')), may hold values from -0.059814453 to 0.059814453
- expert_ids: int32 [262144, 1], P(('expert', 'fsdp')), may hold values from 0 to 15; in each aligned block of 256 rows (0 to 255, 256 to 511, ...) at most 24 rows name the same one
- route_gates: float32 [262144, 1], P(('expert', 'fsdp')), may hold values from 0.2 to 1
- hidden_saved: bfloat16 [16, 64, 16, 24, 768], P('expert', 'fsdp'), may hold values from -6 to 6
- momentum: float32 [16, 2048, 768], P('expert', 'fsdp'), may hold values from -30 to 30
Outputs:
- new_momentum: float32 [16, 2048, 768], P('expert', 'fsdp')
- update: float32 [16, 2048, 768], P('expert', 'fsdp')
The draws below stay inside these ranges and needn't reach their ends.
Inputs may be any that keep to these rules, and one draw needn't show every extreme that they name: `expert_ids`: in each aligned block of 256 tokens (the tokens of one device) no expert is named by more than 24 routes, and in some block one expert is named by exactly 24.
All inputs are finite; a program needn't handle non-finite values.
Results may differ from the reference program's by a relative error of at most 0.0028.
Values may be sent and summed in bfloat16 or wider, within the bound.
No kernel may reach another device: no remote copies, remote signals or barrier semaphores. Data moves between devices by JAX's collectives and lax.ppermute only.
A program may use at most 32 MiB of HBM per device.

```python
import math
import jax
import jax.numpy as jnp
import numpy as np
from jax import lax

D = 2048
FF = 768
ROUTES = 1
TOK_DEV = 256
EXPERT_WAYS = 16
FSDP_WAYS = 64
EXPERTS = 16
CAP = 24
TOKENS = 262144
N_EXPERT = 16
N_FSDP = 64


def draw_momentum(key, part):
    first_key, second_key, third_key = jax.random.split(jax.random.fold_in(key, 7), 3)
    rising = jnp.arange(D, dtype=jnp.float32) / D
    row_scale = 10.0 ** (0.5 * rising[None, :, None] + 0.5 * jax.random.uniform(second_key, (EXPERTS, D, 1), jnp.float32))
    column_scale = 10.0 ** jax.random.uniform(third_key, (EXPERTS, 1, FF), jnp.float32)
    base = jnp.clip(jax.random.normal(first_key, (EXPERTS, D, FF), jnp.float32), -6.0, 6.0)
    overall = 0.05
    return overall * base * row_scale * column_scale


def block_scale(key, dims, cuts, low, top_value):
    level = 1.0
    for dim, blocks in cuts:
        draws = jax.random.uniform(jax.random.fold_in(jax.random.fold_in(key, 6), dim), (blocks,), jnp.float32, low / len(cuts), top_value / len(cuts))
        level = level * jnp.repeat(jnp.exp(draws), dims[dim] // blocks).reshape((-1,) + (1,) * (len(dims) - 1 - dim))
    return level


def routed_block(key, own, number, rows, amount, top, most, slope):
    sequence = jax.random.permutation(key, amount)
    packed, ordinary = portions_of(amount, rows * top, most, slope, True), portions_of(amount, rows * top, most, slope, False)
    places = jnp.arange(amount)

    def named(lengths, offset_by):
        used = int((lengths > 0).sum())
        fixed = max(1, used // 4)
        passed = fixed + (places - fixed + offset_by * (used - fixed)) % max(1, amount - fixed)
        return jnp.zeros((amount,), jnp.int32).at[sequence[jnp.where(places < fixed, places, passed)]].set(jnp.asarray(lengths, jnp.int32))

    lengths = jnp.where(number % 4 == 0, named(packed, number // 4), named(ordinary, number - number // 4 - 1))
    mixed = jax.random.permutation(jax.random.fold_in(own, 3), amount)
    source_of, receiver = mixed[0:amount // 2 * 2:2], mixed[1:amount // 2 * 2:2]
    margin = jnp.minimum(lengths[source_of] - 1, most - lengths[receiver]) // 2
    margin = jnp.where((source_of == sequence[0]) | (receiver == sequence[0]) | (lengths[receiver] == 0), 0, jnp.maximum(margin, 0))
    passed = jax.random.randint(jax.random.fold_in(own, 4), (amount // 2,), 0, 1 << 20) % (margin + 1)
    lengths = lengths.at[source_of].add(-passed).at[receiver].add(passed)
    members = jnp.searchsorted(jnp.cumsum(lengths), jnp.arange(rows * top), side="right").astype(jnp.int32)
    table = members.reshape(top, rows).T
    table = table[jax.random.permutation(jax.random.fold_in(own, 1), rows)]
    offset_by = jax.random.randint(jax.random.fold_in(own, 2), (rows, 1), 0, top)
    return jnp.take_along_axis(table, (jnp.arange(top)[None, :] + offset_by) % top, axis=1)


def portions_of(count, total, reach, lean, full):
    loads = [(1 << 20) // math.isqrt(standing ** lean) + 1 for standing in range(1, count + 1)]
    largest = reach if full else min(reach, max(-(-total // count), total * loads[0] // sum(loads)))
    least = 1 if total - largest >= count - 1 else 0
    counts, spare = [largest] + [least] * (count - 1), total - largest - least * (count - 1)
    while spare > 0:
        free = [i for i in range(1, count) if counts[i] < largest] or [i for i in range(1, count) if counts[i] < reach]
        pool, left = sum([loads[i] for i in free]), spare
        for i in free:
            extra = min(reach - counts[i], max(1, left * loads[i] // pool), spare)
            counts[i] = counts[i] + extra
            spare = spare - extra
    return np.array(counts)


def scatter_about(stream_key, dims, scale, bound, pieces=(), kind=jnp.bfloat16):
    loudness = block_scale(stream_key, dims, pieces, -0.22, 0.18) if pieces else 1.0
    entries = jax.random.normal(stream_key, dims, jnp.float32) * scale * loudness
    return jnp.minimum(jnp.maximum(entries, -bound), bound).astype(kind)


def setup_inputs(seed: int = 0) -> dict:
    key_list = jax.random.split(jax.random.key(seed), 6)
    out_grad = scatter_about(key_list[0], (TOKENS, D), 0.01, 0.059814453, ((0, 1024),))
    expert_ids_keys = jax.random.split(jax.random.fold_in(key_list[1], 1), TOKENS // TOK_DEV)
    expert_ids_turns = jax.random.permutation(jax.random.fold_in(key_list[1], 3), TOKENS // TOK_DEV)
    expert_ids = jax.vmap(lambda own, number: routed_block(jax.random.fold_in(key_list[1], 2), own, number, TOK_DEV, EXPERTS, ROUTES, CAP, 2))(expert_ids_keys, expert_ids_turns).reshape((TOKENS, ROUTES))
    route_gates = jnp.clip(0.2 + 0.8 * jax.random.uniform(key_list[2], (TOKENS, ROUTES), jnp.float32) ** block_scale(key_list[2], (TOKENS, ROUTES), ((0, 1024),), -0.2, 0.2), 0.2, 1.0)
    hidden_saved = scatter_about(key_list[3], (EXPERTS, FSDP_WAYS, EXPERT_WAYS, CAP, FF), 1.0, 6.0, ((0, 16), (1, 64)))
    momentum = draw_momentum(jax.random.fold_in(key_list[5], 71), 0)
    return dict(out_grad=out_grad, expert_ids=expert_ids, route_gates=route_gates, hidden_saved=hidden_saved, momentum=momentum)


QUINTIC = (3.4445, -4.775, 2.0315)
DECAY = 0.95
EPSILON = 1e-07

def slot_numbers(expert_ids):
    flat_ids = expert_ids.reshape(-1).astype(jnp.int32)
    one_hot = (flat_ids[:, None] == jnp.arange(EXPERTS, dtype=jnp.int32)[None, :]).astype(jnp.int32)
    grouped = one_hot.reshape(-1, TOK_DEV * ROUTES, EXPERTS)
    order_rank = jnp.cumsum(grouped, axis=1) - grouped
    slot_index = lax.optimization_barrier(jnp.sum(order_rank * grouped, axis=2)).reshape(-1)
    return (flat_ids, slot_index)

def polynomial(matrix, gram):
    first = jnp.dot(matrix, gram, precision=lax.Precision.HIGHEST)
    second = jnp.dot(first, gram, precision=lax.Precision.HIGHEST)
    return QUINTIC[0] * matrix + QUINTIC[1] * first + QUINTIC[2] * second

def reference(out_grad, expert_ids, route_gates, hidden_saved, momentum):
    routed = (route_gates[:, :, None] * out_grad[:, None, :].astype(jnp.float32)).astype(jnp.bfloat16)
    routed = routed.reshape(-1, D)
    flat_ids, slot_index = slot_numbers(expert_ids)
    device = jnp.arange(flat_ids.shape[0], dtype=jnp.int32) // (TOK_DEV * ROUTES)
    source = device // N_FSDP
    fsdp_index = device % N_FSDP
    target = ((flat_ids * N_FSDP + fsdp_index) * N_EXPERT + source) * CAP + slot_index
    capacity = jnp.zeros((EXPERTS * N_FSDP * N_EXPERT * CAP, D), jnp.bfloat16).at[target].set(routed)
    capacity = capacity.reshape(EXPERTS, N_FSDP * N_EXPERT * CAP, D)
    hidden = hidden_saved.reshape(EXPERTS, N_FSDP * N_EXPERT * CAP, FF)

    def single(operands):
        rows_in, hidden_rows, moment = operands
        gradient = jnp.dot(rows_in.T, hidden_rows, preferred_element_type=jnp.float32)
        moment_new = DECAY * moment + gradient
        velocity = gradient + DECAY * moment_new
        square_sum = jnp.sum(velocity * velocity) + EPSILON
        start_x = velocity / jnp.sqrt(square_sum)
        gram_zero = jnp.dot(start_x.T, start_x, precision=lax.Precision.HIGHEST)
        next_x = polynomial(start_x, gram_zero)
        gram_one = jnp.dot(next_x.T, next_x, precision=lax.Precision.HIGHEST)
        final_x = polynomial(next_x, gram_one)
        return (moment_new, final_x * jnp.sqrt(jnp.float32(D)))
    new_momentum, update = lax.map(single, (capacity, hidden, momentum))
    return (new_momentum, update)
```

```python
import jax
import jax.numpy as jnp
from jax import lax
from jax.experimental import pallas as pl
from jax.experimental.pallas import tpu as pltpu
from jax.sharding import Mesh
from jax.sharding import PartitionSpec as P

D = 2048
FSDP = ("z", "core")
EXPERT_FSDP = ("expert", "z", "core")

QUINTIC = (3.4445, -4.775, 2.0315)
DECAY = 0.95
EPSILON = 1e-07

STRIDE = 3
REACH = 5
FAR = range(-REACH, REACH + 1)
UP = tuple(a for a in FAR if a < REACH)
DOWN = tuple(FAR)
OFFSETS = (
    tuple(STRIDE * a + 1 for a in UP)
    + tuple(STRIDE * a - 1 for a in DOWN)
    + tuple(STRIDE * a for a in FAR)
)
NARROW = (5, 4)


def shifted(x, by, ring):
    return lax.ppermute(x, "z", [(i, (i + by) % ring) for i in range(ring)])


def swapped(x):
    return lax.ppermute(x, "core", [(0, 1), (1, 0)])


def route_kernel(ids_ref, gates_ref, grad_ref, out_ref, *, experts, capacity):
    rows, features = grad_ref.shape
    slots = experts * capacity
    f32, bf16 = jnp.float32, jnp.bfloat16
    ids = ids_ref[...]
    one_hot = lax.broadcasted_iota(jnp.int32, (experts, rows), 0) == ids
    one_hot = jnp.where(one_hot, 1.0, 0.0).astype(f32)
    r = lax.broadcasted_iota(jnp.int32, (rows, rows), 0)
    c = lax.broadcasted_iota(jnp.int32, (rows, rows), 1)
    earlier = jnp.where(r < c, 1.0, 0.0).astype(bf16)
    rank = jnp.dot(one_hot.astype(bf16), earlier, preferred_element_type=f32)
    slot = jnp.sum(rank * one_hot, axis=0, keepdims=True)
    target = ids.astype(f32) * float(capacity) + slot
    place = lax.broadcasted_iota(jnp.int32, (slots, rows), 0).astype(f32)
    placing = jnp.where(place == target, 1.0, 0.0).astype(bf16)
    gates = jnp.transpose(jnp.broadcast_to(gates_ref[...], (128, rows)))[:, 0:1]
    routed = (gates * grad_ref[...].astype(f32)).astype(bf16)
    src = lax.broadcasted_iota(jnp.int32, (256, 256), 0)
    dst = lax.broadcasted_iota(jnp.int32, (256, 256), 1)
    wanted = (dst % 128 // 32) * 64 + (dst // 128) * 32 + dst % 32
    sorting = jnp.where(src == wanted, 1.0, 0.0).astype(bf16)
    for block in range(features // 256):
        columns = routed[:, block * 256 : (block + 1) * 256]
        columns = jnp.dot(columns, sorting, preferred_element_type=f32).astype(bf16)
        placed = jnp.dot(placing, columns, preferred_element_type=f32)
        for e in range(experts):
            piece = placed[e * capacity : (e + 1) * capacity].astype(bf16)
            for core in range(2):
                out_ref[2 * e + core, :, block * 128 : (block + 1) * 128] = piece[
                    :, core * 128 : (core + 1) * 128
                ]


def partial_kernel(chunk_ref, rows_ref, hidden_ref, up_ref, down_ref, middle_ref, part_ref):
    _, size, _ = part_ref.shape
    hidden = hidden_ref[...]
    for block in range(rows_ref.shape[1] // 256):
        part = lax.dot_general(
            rows_ref[:, block * 256 : (block + 1) * 256],
            hidden,
            (((0,), (0,)), ((), ())),
            preferred_element_type=jnp.float32,
        )
        for k in range(256 // size):
            part_ref[block * (256 // size) + k] = part[k * size : (k + 1) * size]
    at = 0
    for ref in (up_ref, down_ref, middle_ref):
        for i in range(ref.shape[0]):
            ref[i] = part_ref[chunk_ref[at]].astype(ref.dtype)
            at += 1


def newton_kernel(velocity_ref, own_ref, other_ref, out_ref, gram_ref):
    f32, bf16 = jnp.float32, jnp.bfloat16
    units = own_ref.shape[0]
    rows = velocity_ref.shape[0]
    trace = jnp.zeros((1, 128), f32)
    eye = lax.broadcasted_iota(jnp.int32, (128, 128), 0) == lax.broadcasted_iota(
        jnp.int32, (128, 128), 1
    )
    for i in range(units // 128):
        at = slice(i * 128, (i + 1) * 128)
        tile = own_ref[at, at] + other_ref[at, at].astype(f32)
        trace = trace + jnp.sum(jnp.where(eye, tile, 0.0), axis=0, keepdims=True)
    square_sum = jnp.sum(trace, axis=1, keepdims=True) + EPSILON
    inverse = 1.0 / square_sum
    gram_ref[...] = ((own_ref[...] + other_ref[...].astype(f32)) * inverse).astype(bf16)
    gram = gram_ref[...]

    def times(x):
        high = x.astype(bf16)
        low = (x - high.astype(f32)).astype(bf16)
        both = jnp.dot(
            jnp.concatenate([high, low], axis=0), gram, preferred_element_type=f32
        )
        return both[:rows] + both[rows:]

    def apply_first(x):
        once = times(x)
        return QUINTIC[0] * x + QUINTIC[1] * once + QUINTIC[2] * times(once)

    def apply_second(x):
        return apply_first(times(apply_first(x)))

    start = velocity_ref[...] / jnp.sqrt(square_sum)
    first = apply_first(start)
    once_more = apply_second(first)
    twice_more = apply_second(once_more)
    final = QUINTIC[0] * first + QUINTIC[1] * once_more + QUINTIC[2] * twice_more
    out_ref[...] = final * jnp.sqrt(jnp.float32(D))


def after(x, earlier):
    return lax.optimization_barrier((x, earlier))[0]


def reduce_over_ring(up, down, middle, ring):
    f32, bf16 = jnp.float32, jnp.bfloat16
    up = shifted(up, -1, ring)
    down = shifted(down, 1, ring)
    sums = {}
    for n, a in enumerate(FAR):
        sums[a] = middle[n] + down[DOWN.index(a)].astype(f32)
        if a in UP:
            sums[a] = sums[a] + up[UP.index(a)].astype(f32)
    sums = lax.optimization_barrier(sums)
    got = {}
    last = None
    for k in range(REACH, 0, -1):
        for side in (1, -1):
            total = sums[side * k]
            if side in got:
                total = total + after(got[side], last).astype(f32)
            last = total.astype(bf16 if k in NARROW else f32)
            got[side] = shifted(last, -side * STRIDE, ring)
    return sums[0] + got[1].astype(f32) + got[-1].astype(f32)


def gram_of(blocks):
    flat = blocks.reshape(-1, blocks.shape[-1])
    return lax.dot_general(
        flat, flat, (((0,), (0,)), ((), ())), preferred_element_type=jnp.float32
    )


def gram_over_ring(own, ring):
    held = {0: own}
    for k in range(1, REACH + 1):
        for side in (1, -1):
            held[side * k] = shifted(held[side * (k - 1)], -side * STRIDE, ring)
    rows = jnp.stack([held[a] for a in FAR])
    up = shifted(rows[: len(UP)], -1, ring)
    down = shifted(rows, 1, ring)
    return gram_of(rows) + gram_of(up) + gram_of(down)


def local(out_grad, expert_ids, route_gates, hidden_saved, momentum):
    f32, bf16 = jnp.float32, jnp.bfloat16
    n_expert = lax.axis_size("expert")
    ring = lax.axis_size("z")
    z = lax.axis_index("z")
    core = lax.axis_index("core")
    _, d_local, units = momentum.shape
    tok_rows, features = out_grad.shape
    capacity = hidden_saved.shape[3]
    half = features // 2
    own_hidden = hidden_saved.reshape(n_expert, capacity, units)
    other_hidden = swapped(own_hidden)
    outgoing = pl.pallas_call(
        lambda *refs: route_kernel(*refs, experts=n_expert, capacity=capacity),
        out_shape=jax.ShapeDtypeStruct((2 * n_expert, capacity, half), bf16),
        name="route",
    )(expert_ids.reshape(1, tok_rows), route_gates.reshape(1, tok_rows), out_grad)
    received = lax.all_to_all(
        outgoing, ("expert", "core"), split_axis=0, concat_axis=0, tiled=True
    )
    rows = received.reshape(2 * n_expert * capacity, half)
    first_core = core == 0
    hidden = jnp.stack(
        [
            jnp.where(first_core, own_hidden, other_hidden),
            jnp.where(first_core, other_hidden, own_hidden),
        ],
        axis=1,
    ).reshape(2 * n_expert * capacity, units)
    chunk = (z - jnp.array(OFFSETS, dtype=jnp.int32)) % ring
    up, down, middle = pl.pallas_call(
        partial_kernel,
        out_shape=(
            jax.ShapeDtypeStruct((len(UP), d_local, units), bf16),
            jax.ShapeDtypeStruct((len(DOWN), d_local, units), bf16),
            jax.ShapeDtypeStruct((len(FAR), d_local, units), f32),
        ),
        in_specs=[
            pl.BlockSpec(memory_space=pltpu.SMEM),
            pl.BlockSpec(memory_space=pltpu.VMEM),
            pl.BlockSpec(memory_space=pltpu.VMEM),
        ],
        out_specs=(
            pl.BlockSpec(memory_space=pltpu.VMEM),
            pl.BlockSpec(memory_space=pltpu.VMEM),
            pl.BlockSpec(memory_space=pltpu.VMEM),
        ),
        scratch_shapes=[pltpu.VMEM((ring, d_local, units), f32)],
        name="partial",
    )(chunk, rows, hidden)
    gradient = reduce_over_ring(up, down, middle, ring)
    moment_new = DECAY * momentum[0] + gradient
    velocity = gradient + DECAY * moment_new
    gram = gram_over_ring(velocity.astype(bf16), ring)
    other_gram = swapped(gram.astype(bf16))
    update = pl.pallas_call(
        newton_kernel,
        out_shape=jax.ShapeDtypeStruct((d_local, units), f32),
        scratch_shapes=[pltpu.VMEM((units, units), bf16)],
        name="newton",
    )(velocity, gram, other_gram)
    return moment_new[None], update[None]


def solution(mesh):
    finer = Mesh(
        mesh.devices.reshape(mesh.shape["expert"], mesh.shape["fsdp"] // 2, 2), EXPERT_FSDP
    )
    placed = (
        P(EXPERT_FSDP, None),
        P(EXPERT_FSDP, None),
        P(EXPERT_FSDP, None),
        P("expert", FSDP, None, None, None),
        P("expert", FSDP, None),
    )
    return jax.shard_map(
        local,
        mesh=finer,
        in_specs=placed,
        out_specs=(P("expert", FSDP, None), P("expert", FSDP, None)),
        check_vma=False,
    )
```

```python
import jax
import jax.numpy as jnp
from jax import lax
from jax.experimental import pallas as pl
from jax.experimental.pallas import tpu as pltpu
from jax.sharding import Mesh
from jax.sharding import PartitionSpec as P

D = 2048
FSDP = ("z", "core")
EXPERT_FSDP = ("expert", "z", "core")

QUINTIC = (3.4445, -4.775, 2.0315)
DECAY = 0.95
EPSILON = 1e-07

STRIDE = 3
REACH = 5
FAR = range(-REACH, REACH + 1)
UP = tuple(a for a in FAR if a < REACH)
DOWN = tuple(FAR)
OFFSETS = (
    tuple(STRIDE * a + 1 for a in UP)
    + tuple(STRIDE * a - 1 for a in DOWN)
    + tuple(STRIDE * a for a in FAR)
)

def shifted(x, by, ring):
    return lax.ppermute(x, "z", [(i, (i + by) % ring) for i in range(ring)])


def swapped(x):
    return lax.ppermute(x, "core", [(0, 1), (1, 0)])


def route_kernel(ids_ref, gates_ref, grad_ref, out_ref, *, experts, capacity):
    rows, features = grad_ref.shape
    slots = experts * capacity
    f32, bf16 = jnp.float32, jnp.bfloat16
    ids = ids_ref[...]
    one_hot = lax.broadcasted_iota(jnp.int32, (experts, rows), 0) == ids
    one_hot = jnp.where(one_hot, 1.0, 0.0).astype(f32)
    r = lax.broadcasted_iota(jnp.int32, (rows, rows), 0)
    c = lax.broadcasted_iota(jnp.int32, (rows, rows), 1)
    earlier = jnp.where(r < c, 1.0, 0.0).astype(bf16)
    rank = jnp.dot(one_hot.astype(bf16), earlier, preferred_element_type=f32)
    slot = jnp.sum(rank * one_hot, axis=0, keepdims=True)
    target = ids.astype(f32) * float(capacity) + slot
    place = lax.broadcasted_iota(jnp.int32, (slots, rows), 0).astype(f32)
    placing = jnp.where(place == target, 1.0, 0.0).astype(bf16)
    gates = jnp.transpose(jnp.broadcast_to(gates_ref[...], (128, rows)))[:, 0:1]
    routed = (gates * grad_ref[...].astype(f32)).astype(bf16)
    src = lax.broadcasted_iota(jnp.int32, (256, 256), 0)
    dst = lax.broadcasted_iota(jnp.int32, (256, 256), 1)
    wanted = (dst % 128 // 32) * 64 + (dst // 128) * 32 + dst % 32
    sorting = jnp.where(src == wanted, 1.0, 0.0).astype(bf16)
    for block in range(features // 256):
        columns = routed[:, block * 256 : (block + 1) * 256]
        columns = jnp.dot(columns, sorting, preferred_element_type=f32).astype(bf16)
        placed = jnp.dot(placing, columns, preferred_element_type=f32)
        for e in range(experts):
            piece = placed[e * capacity : (e + 1) * capacity].astype(bf16)
            for core in range(2):
                out_ref[2 * e + core, :, block * 128 : (block + 1) * 128] = piece[
                    :, core * 128 : (core + 1) * 128
                ]


def partial_kernel(chunk_ref, rows_ref, hidden_ref, up_ref, down_ref, middle_ref, part_ref):
    _, size, _ = part_ref.shape
    hidden = hidden_ref[...]
    for block in range(rows_ref.shape[1] // 256):
        part = lax.dot_general(
            rows_ref[:, block * 256 : (block + 1) * 256],
            hidden,
            (((0,), (0,)), ((), ())),
            preferred_element_type=jnp.float32,
        )
        for k in range(256 // size):
            part_ref[block * (256 // size) + k] = part[k * size : (k + 1) * size]
    at = 0
    for ref in (up_ref, down_ref, middle_ref):
        for i in range(ref.shape[0]):
            ref[i] = part_ref[chunk_ref[at]].astype(ref.dtype)
            at += 1


def newton_kernel(velocity_ref, own_ref, other_ref, out_ref, gram_ref):
    f32, bf16 = jnp.float32, jnp.bfloat16
    units = own_ref.shape[0]
    rows = velocity_ref.shape[0]
    trace = jnp.zeros((1, 128), f32)
    eye = lax.broadcasted_iota(jnp.int32, (128, 128), 0) == lax.broadcasted_iota(
        jnp.int32, (128, 128), 1
    )
    for i in range(units // 128):
        at = slice(i * 128, (i + 1) * 128)
        tile = own_ref[at, at].astype(f32) + other_ref[at, at].astype(f32)
        trace = trace + jnp.sum(jnp.where(eye, tile, 0.0), axis=0, keepdims=True)
    square_sum = jnp.sum(trace, axis=1, keepdims=True) + EPSILON
    inverse = 1.0 / square_sum
    whole = own_ref[...].astype(f32) + other_ref[...].astype(f32)
    gram_ref[...] = (whole * inverse).astype(bf16)
    gram = gram_ref[...]

    def times(x):
        high = x.astype(bf16)
        low = (x - high.astype(f32)).astype(bf16)
        both = jnp.dot(
            jnp.concatenate([high, low], axis=0), gram, preferred_element_type=f32
        )
        return both[:rows] + both[rows:]

    def apply_first(x):
        once = times(x)
        return QUINTIC[0] * x + QUINTIC[1] * once + QUINTIC[2] * times(once)

    def apply_second(x):
        return apply_first(times(apply_first(x)))

    start = velocity_ref[...] / jnp.sqrt(square_sum)
    first = apply_first(start)
    once_more = apply_second(first)
    twice_more = apply_second(once_more)
    final = QUINTIC[0] * first + QUINTIC[1] * once_more + QUINTIC[2] * twice_more
    out_ref[...] = final * jnp.sqrt(jnp.float32(D))


def after(x, earlier):
    return lax.optimization_barrier((x, earlier))[0]


def reduce_over_ring(up, down, middle, ring):
    f32 = jnp.float32
    up = shifted(up, -1, ring)
    down = shifted(down, 1, ring)
    sums = {}
    for n, a in enumerate(FAR):
        sums[a] = middle[n] + down[DOWN.index(a)].astype(f32)
        if a in UP:
            sums[a] = sums[a] + up[UP.index(a)].astype(f32)
    sums = lax.optimization_barrier(sums)
    got = {}
    last = None
    for k in range(REACH, 0, -1):
        for side in (1, -1):
            total = sums[side * k]
            if side in got:
                total = total + after(got[side], last)
            last = total
            got[side] = shifted(total, -side * STRIDE, ring)
    return sums[0] + got[1] + got[-1]


def gram_of(blocks):
    flat = blocks.reshape(-1, blocks.shape[-1])
    return lax.dot_general(
        flat, flat, (((0,), (0,)), ((), ())), preferred_element_type=jnp.float32
    )


def gram_over_ring(own, ring):
    held = {0: own}
    for k in range(1, REACH + 1):
        for side in (1, -1):
            held[side * k] = shifted(held[side * (k - 1)], -side * STRIDE, ring)
    rows = lax.optimization_barrier(jnp.stack([held[a] for a in FAR]))
    up = shifted(rows[: len(UP)], -1, ring)
    down = shifted(rows, 1, ring)
    return gram_of(rows) + gram_of(up) + gram_of(down)


def local(out_grad, expert_ids, route_gates, hidden_saved, momentum):
    f32, bf16 = jnp.float32, jnp.bfloat16
    n_expert = lax.axis_size("expert")
    ring = lax.axis_size("z")
    z = lax.axis_index("z")
    core = lax.axis_index("core")
    _, d_local, units = momentum.shape
    tok_rows, features = out_grad.shape
    capacity = hidden_saved.shape[3]
    half = features // 2
    own_hidden = hidden_saved.reshape(n_expert, capacity, units)
    other_hidden = swapped(own_hidden)
    outgoing = pl.pallas_call(
        lambda *refs: route_kernel(*refs, experts=n_expert, capacity=capacity),
        out_shape=jax.ShapeDtypeStruct((2 * n_expert, capacity, half), bf16),
        name="route",
    )(expert_ids.reshape(1, tok_rows), route_gates.reshape(1, tok_rows), out_grad)
    received = lax.all_to_all(
        outgoing, ("expert", "core"), split_axis=0, concat_axis=0, tiled=True
    )
    rows = received.reshape(2 * n_expert * capacity, half)
    first_core = core == 0
    hidden = jnp.stack(
        [
            jnp.where(first_core, own_hidden, other_hidden),
            jnp.where(first_core, other_hidden, own_hidden),
        ],
        axis=1,
    ).reshape(2 * n_expert * capacity, units)
    chunk = (z - jnp.array(OFFSETS, dtype=jnp.int32)) % ring
    up, down, middle = pl.pallas_call(
        partial_kernel,
        out_shape=(
            jax.ShapeDtypeStruct((len(UP), d_local, units), bf16),
            jax.ShapeDtypeStruct((len(DOWN), d_local, units), bf16),
            jax.ShapeDtypeStruct((len(FAR), d_local, units), f32),
        ),
        in_specs=[
            pl.BlockSpec(memory_space=pltpu.SMEM),
            pl.BlockSpec(memory_space=pltpu.VMEM),
            pl.BlockSpec(memory_space=pltpu.VMEM),
        ],
        out_specs=(
            pl.BlockSpec(memory_space=pltpu.VMEM),
            pl.BlockSpec(memory_space=pltpu.VMEM),
            pl.BlockSpec(memory_space=pltpu.VMEM),
        ),
        scratch_shapes=[pltpu.VMEM((ring, d_local, units), f32)],
        name="partial",
    )(chunk, rows, hidden)
    gradient = reduce_over_ring(up, down, middle, ring)
    moment_new = DECAY * momentum[0] + gradient
    velocity = gradient + DECAY * moment_new
    gram = gram_over_ring(velocity.astype(bf16), ring).astype(bf16)
    other_gram = swapped(gram)
    update = pl.pallas_call(
        newton_kernel,
        out_shape=jax.ShapeDtypeStruct((d_local, units), f32),
        scratch_shapes=[pltpu.VMEM((units, units), bf16)],
        name="newton",
    )(velocity, gram, other_gram)
    return moment_new[None], update[None]


def solution(mesh):
    finer = Mesh(
        mesh.devices.reshape(mesh.shape["expert"], mesh.shape["fsdp"] // 2, 2), EXPERT_FSDP
    )
    placed = (
        P(EXPERT_FSDP, None),
        P(EXPERT_FSDP, None),
        P(EXPERT_FSDP, None),
        P("expert", FSDP, None, None, None),
        P("expert", FSDP, None),
    )
    return jax.shard_map(
        local,
        mesh=finer,
        in_specs=placed,
        out_specs=(P("expert", FSDP, None), P("expert", FSDP, None)),
        check_vma=False,
    )
```

```python
import jax
import jax.numpy as jnp
from jax import lax
from jax.experimental import pallas as pl
from jax.experimental.pallas import tpu as pltpu
from jax.sharding import Mesh
from jax.sharding import PartitionSpec as P

D = 2048
FSDP = ("z", "core")
EXPERT_FSDP = ("expert", "z", "core")

QUINTIC = (3.4445, -4.775, 2.0315)
DECAY = 0.95
EPSILON = 1e-07

STRIDE = 3
BASE = (0, 3, -3)
ABOVE = (1, 4, -2)
BELOW = (-1, 2, -4)
STEPS = BASE + ABOVE + BELOW + (-5, 5)
UP = STEPS[:-1]
DOWN = STEPS
OFFSETS = (
    tuple(STRIDE * a + 1 for a in UP)
    + tuple(STRIDE * a - 1 for a in DOWN)
    + tuple(STRIDE * a for a in STEPS)
)


def shifted(x, by, ring):
    return lax.ppermute(x, "z", [(i, (i + by) % ring) for i in range(ring)])


def swapped(x):
    return lax.ppermute(x, "core", [(0, 1), (1, 0)])


def route_kernel(ids_ref, gates_ref, grad_ref, out_ref, *, experts, capacity):
    rows, features = grad_ref.shape
    slots = experts * capacity
    f32, bf16 = jnp.float32, jnp.bfloat16
    ids = ids_ref[...]
    one_hot = lax.broadcasted_iota(jnp.int32, (experts, rows), 0) == ids
    one_hot = jnp.where(one_hot, 1.0, 0.0).astype(f32)
    r = lax.broadcasted_iota(jnp.int32, (rows, rows), 0)
    c = lax.broadcasted_iota(jnp.int32, (rows, rows), 1)
    earlier = jnp.where(r < c, 1.0, 0.0).astype(bf16)
    rank = jnp.dot(one_hot.astype(bf16), earlier, preferred_element_type=f32)
    slot = jnp.sum(rank * one_hot, axis=0, keepdims=True)
    target = ids.astype(f32) * float(capacity) + slot
    place = lax.broadcasted_iota(jnp.int32, (slots, rows), 0).astype(f32)
    placing = jnp.where(place == target, 1.0, 0.0).astype(bf16)
    gates = jnp.transpose(jnp.broadcast_to(gates_ref[...], (128, rows)))[:, 0:1]
    routed = (gates * grad_ref[...].astype(f32)).astype(bf16)
    src = lax.broadcasted_iota(jnp.int32, (256, 256), 0)
    dst = lax.broadcasted_iota(jnp.int32, (256, 256), 1)
    wanted = (dst % 128 // 32) * 64 + (dst // 128) * 32 + dst % 32
    sorting = jnp.where(src == wanted, 1.0, 0.0).astype(bf16)
    for block in range(features // 256):
        columns = routed[:, block * 256 : (block + 1) * 256]
        columns = jnp.dot(columns, sorting, preferred_element_type=f32).astype(bf16)
        placed = jnp.dot(placing, columns, preferred_element_type=f32)
        for e in range(experts):
            piece = placed[e * capacity : (e + 1) * capacity].astype(bf16)
            for core in range(2):
                out_ref[2 * e + core, :, block * 128 : (block + 1) * 128] = piece[
                    :, core * 128 : (core + 1) * 128
                ]


def partial_kernel(chunk_ref, rows_ref, hidden_ref, up_ref, down_ref, middle_ref, part_ref):
    _, size, _ = part_ref.shape
    hidden = hidden_ref[...]
    for block in range(rows_ref.shape[1] // 256):
        part = lax.dot_general(
            rows_ref[:, block * 256 : (block + 1) * 256],
            hidden,
            (((0,), (0,)), ((), ())),
            preferred_element_type=jnp.float32,
        )
        for k in range(256 // size):
            part_ref[block * (256 // size) + k] = part[k * size : (k + 1) * size]
    at = 0
    for ref in (up_ref, down_ref, middle_ref):
        for i in range(ref.shape[0]):
            ref[i] = part_ref[chunk_ref[at]].astype(ref.dtype)
            at += 1


def newton_kernel(velocity_ref, own_ref, other_ref, out_ref, gram_ref):
    f32, bf16 = jnp.float32, jnp.bfloat16
    units = own_ref.shape[0]
    rows = velocity_ref.shape[0]
    trace = jnp.zeros((1, 128), f32)
    eye = lax.broadcasted_iota(jnp.int32, (128, 128), 0) == lax.broadcasted_iota(
        jnp.int32, (128, 128), 1
    )
    for i in range(units // 128):
        at = slice(i * 128, (i + 1) * 128)
        tile = own_ref[at, at].astype(f32) + other_ref[at, at].astype(f32)
        trace = trace + jnp.sum(jnp.where(eye, tile, 0.0), axis=0, keepdims=True)
    square_sum = jnp.sum(trace, axis=1, keepdims=True) + EPSILON
    inverse = 1.0 / square_sum
    whole = own_ref[...].astype(f32) + other_ref[...].astype(f32)
    gram_ref[...] = (whole * inverse).astype(bf16)
    gram = gram_ref[...]

    def times(x):
        high = x.astype(bf16)
        low = (x - high.astype(f32)).astype(bf16)
        both = jnp.dot(
            jnp.concatenate([high, low], axis=0), gram, preferred_element_type=f32
        )
        return both[:rows] + both[rows:]

    def apply_first(x):
        once = times(x)
        return QUINTIC[0] * x + QUINTIC[1] * once + QUINTIC[2] * times(once)

    def apply_second(x):
        return apply_first(times(apply_first(x)))

    start = velocity_ref[...] / jnp.sqrt(square_sum)
    first = apply_first(start)
    once_more = apply_second(first)
    twice_more = apply_second(once_more)
    final = QUINTIC[0] * first + QUINTIC[1] * once_more + QUINTIC[2] * twice_more
    out_ref[...] = final * jnp.sqrt(jnp.float32(D))


def reduce_over_ring(up, down, middle, ring):
    f32, bf16 = jnp.float32, jnp.bfloat16
    up = shifted(up, -1, ring)
    down = shifted(down, 1, ring)
    sums = middle + down.astype(f32)
    sums = jnp.concatenate([sums[:-1] + up.astype(f32), sums[-1:]])
    sums = lax.optimization_barrier(sums)
    base, above, below = sums[0:3], sums[3:6], sums[6:9]
    up = shifted(sums[10].astype(bf16), -STRIDE, ring).astype(f32)
    down = shifted(sums[9].astype(bf16), STRIDE, ring).astype(f32)
    above = jnp.stack([above[0], above[1] + up, above[2]]).astype(bf16)
    below = jnp.stack([below[0], below[1], below[2] + down]).astype(bf16)
    above, below = lax.optimization_barrier((above, below))
    up = shifted(above, -STRIDE, ring)
    down = shifted(below, STRIDE, ring)
    base = base + up.astype(f32) + down.astype(f32)
    far = lax.optimization_barrier((base[0], base[1].astype(bf16), base[2].astype(bf16)))
    up = shifted(far[1], -3 * STRIDE, ring)
    down = shifted(far[2], 3 * STRIDE, ring)
    return far[0] + up.astype(f32) + down.astype(f32)


def gram_of(blocks):
    flat = blocks.reshape(-1, blocks.shape[-1])
    return lax.dot_general(
        flat, flat, (((0,), (0,)), ((), ())), preferred_element_type=jnp.float32
    )


def gram_over_ring(own, ring):
    base = jnp.stack([own, shifted(own, -3 * STRIDE, ring), shifted(own, 3 * STRIDE, ring)])
    above = shifted(base, -STRIDE, ring)
    below = shifted(base, STRIDE, ring)
    up = shifted(above[1:2], -STRIDE, ring)
    down = shifted(below[2:3], STRIDE, ring)
    rows = lax.optimization_barrier(jnp.concatenate([base, above, below, down, up]))
    up = shifted(rows[:-1], -1, ring)
    down = shifted(rows, 1, ring)
    return gram_of(rows) + gram_of(up) + gram_of(down)


def local(out_grad, expert_ids, route_gates, hidden_saved, momentum):
    f32, bf16 = jnp.float32, jnp.bfloat16
    n_expert = lax.axis_size("expert")
    ring = lax.axis_size("z")
    z = lax.axis_index("z")
    core = lax.axis_index("core")
    _, d_local, units = momentum.shape
    tok_rows, features = out_grad.shape
    capacity = hidden_saved.shape[3]
    half = features // 2
    own_hidden = hidden_saved.reshape(n_expert, capacity, units)
    other_hidden = swapped(own_hidden)
    outgoing = pl.pallas_call(
        lambda *refs: route_kernel(*refs, experts=n_expert, capacity=capacity),
        out_shape=jax.ShapeDtypeStruct((2 * n_expert, capacity, half), bf16),
        name="route",
    )(expert_ids.reshape(1, tok_rows), route_gates.reshape(1, tok_rows), out_grad)
    received = lax.all_to_all(
        outgoing, ("expert", "core"), split_axis=0, concat_axis=0, tiled=True
    )
    rows = received.reshape(2 * n_expert * capacity, half)
    first_core = core == 0
    hidden = jnp.stack(
        [
            jnp.where(first_core, own_hidden, other_hidden),
            jnp.where(first_core, other_hidden, own_hidden),
        ],
        axis=1,
    ).reshape(2 * n_expert * capacity, units)
    chunk = (z - jnp.array(OFFSETS, dtype=jnp.int32)) % ring
    up, down, middle = pl.pallas_call(
        partial_kernel,
        out_shape=(
            jax.ShapeDtypeStruct((len(UP), d_local, units), bf16),
            jax.ShapeDtypeStruct((len(DOWN), d_local, units), bf16),
            jax.ShapeDtypeStruct((len(STEPS), d_local, units), f32),
        ),
        in_specs=[
            pl.BlockSpec(memory_space=pltpu.SMEM),
            pl.BlockSpec(memory_space=pltpu.VMEM),
            pl.BlockSpec(memory_space=pltpu.VMEM),
        ],
        out_specs=(
            pl.BlockSpec(memory_space=pltpu.VMEM),
            pl.BlockSpec(memory_space=pltpu.VMEM),
            pl.BlockSpec(memory_space=pltpu.VMEM),
        ),
        scratch_shapes=[pltpu.VMEM((ring, d_local, units), f32)],
        name="partial",
    )(chunk, rows, hidden)
    gradient = reduce_over_ring(up, down, middle, ring)
    moment_new = DECAY * momentum[0] + gradient
    velocity = gradient + DECAY * moment_new
    gram = gram_over_ring(velocity.astype(bf16), ring).astype(bf16)
    other_gram = swapped(gram)
    update = pl.pallas_call(
        newton_kernel,
        out_shape=jax.ShapeDtypeStruct((d_local, units), f32),
        scratch_shapes=[pltpu.VMEM((units, units), bf16)],
        name="newton",
    )(velocity, gram, other_gram)
    return moment_new[None], update[None]


def solution(mesh):
    finer = Mesh(
        mesh.devices.reshape(mesh.shape["expert"], mesh.shape["fsdp"] // 2, 2), EXPERT_FSDP
    )
    placed = (
        P(EXPERT_FSDP, None),
        P(EXPERT_FSDP, None),
        P(EXPERT_FSDP, None),
        P("expert", FSDP, None, None, None),
        P("expert", FSDP, None),
    )
    return jax.shard_map(
        local,
        mesh=finer,
        in_specs=placed,
        out_specs=(P("expert", FSDP, None), P("expert", FSDP, None)),
        check_vma=False,
    )
```

```python
import jax
import jax.numpy as jnp
from jax import lax
from jax.experimental import pallas as pl
from jax.experimental.pallas import tpu as pltpu
from jax.sharding import Mesh
from jax.sharding import PartitionSpec as P


D = 2048
FSDP = ("z", "core")
EXPERT_FSDP = ("expert", "z", "core")

QUINTIC = (3.4445, -4.775, 2.0315)
DECAY = 0.95
EPSILON = 1e-07

STRIDE = 3
BASE = (0, 3, -3)
ABOVE = (1, 4, -2)
BELOW = (-1, 2, -4)
STEPS = BASE + ABOVE + BELOW + (-5, 5)
UP = STEPS[:-1]
DOWN = STEPS
REACH = 5
NARROW = (5, 4, 3)
OFFSETS = (
    tuple(STRIDE * a + 1 for a in UP)
    + tuple(STRIDE * a - 1 for a in DOWN)
    + tuple(STRIDE * a for a in STEPS)
)


def shifted(x, by, ring):
    return lax.ppermute(x, "z", [(i, (i + by) % ring) for i in range(ring)])


def swapped(x):
    return lax.ppermute(x, "core", [(0, 1), (1, 0)])


def route_kernel(ids_ref, gates_ref, grad_ref, out_ref, *, experts, capacity):
    rows, features = grad_ref.shape
    slots = experts * capacity
    f32, bf16 = jnp.float32, jnp.bfloat16
    ids = ids_ref[...]
    one_hot = lax.broadcasted_iota(jnp.int32, (experts, rows), 0) == ids
    one_hot = jnp.where(one_hot, 1.0, 0.0).astype(f32)
    r = lax.broadcasted_iota(jnp.int32, (rows, rows), 0)
    c = lax.broadcasted_iota(jnp.int32, (rows, rows), 1)
    earlier = jnp.where(r < c, 1.0, 0.0).astype(bf16)
    rank = jnp.dot(one_hot.astype(bf16), earlier, preferred_element_type=f32)
    slot = jnp.sum(rank * one_hot, axis=0, keepdims=True)
    target = ids.astype(f32) * float(capacity) + slot
    place = lax.broadcasted_iota(jnp.int32, (slots, rows), 0).astype(f32)
    placing = jnp.where(place == target, 1.0, 0.0).astype(bf16)
    gates = jnp.transpose(jnp.broadcast_to(gates_ref[...], (128, rows)))[:, 0:1]
    routed = (gates * grad_ref[...].astype(f32)).astype(bf16)
    src = lax.broadcasted_iota(jnp.int32, (256, 256), 0)
    dst = lax.broadcasted_iota(jnp.int32, (256, 256), 1)
    wanted = (dst % 128 // 32) * 64 + (dst // 128) * 32 + dst % 32
    sorting = jnp.where(src == wanted, 1.0, 0.0).astype(bf16)
    for block in range(features // 256):
        columns = routed[:, block * 256 : (block + 1) * 256]
        columns = jnp.dot(columns, sorting, preferred_element_type=f32).astype(bf16)
        placed = jnp.dot(placing, columns, preferred_element_type=f32)
        for e in range(experts):
            piece = placed[e * capacity : (e + 1) * capacity].astype(bf16)
            for core in range(2):
                out_ref[2 * e + core, :, block * 128 : (block + 1) * 128] = piece[
                    :, core * 128 : (core + 1) * 128
                ]


def partial_kernel(chunk_ref, rows_ref, hidden_ref, up_ref, down_ref, middle_ref, part_ref):
    _, size, _ = part_ref.shape
    hidden = hidden_ref[...]
    for block in range(rows_ref.shape[1] // 256):
        part = lax.dot_general(
            rows_ref[:, block * 256 : (block + 1) * 256],
            hidden,
            (((0,), (0,)), ((), ())),
            preferred_element_type=jnp.float32,
        )
        for k in range(256 // size):
            part_ref[block * (256 // size) + k] = part[k * size : (k + 1) * size]
    at = 0
    for ref in (up_ref, down_ref, middle_ref):
        for i in range(ref.shape[0]):
            ref[i] = part_ref[chunk_ref[at]].astype(ref.dtype)
            at += 1


def newton_kernel(velocity_ref, own_ref, other_ref, out_ref, gram_ref):
    f32, bf16 = jnp.float32, jnp.bfloat16
    units = own_ref.shape[0]
    rows = velocity_ref.shape[0]
    trace = jnp.zeros((1, 128), f32)
    eye = lax.broadcasted_iota(jnp.int32, (128, 128), 0) == lax.broadcasted_iota(
        jnp.int32, (128, 128), 1
    )
    for i in range(units // 128):
        at = slice(i * 128, (i + 1) * 128)
        tile = own_ref[at, at].astype(f32) + other_ref[at, at].astype(f32)
        trace = trace + jnp.sum(jnp.where(eye, tile, 0.0), axis=0, keepdims=True)
    square_sum = jnp.sum(trace, axis=1, keepdims=True) + EPSILON
    inverse = 1.0 / square_sum
    whole = own_ref[...].astype(f32) + other_ref[...].astype(f32)
    gram_ref[...] = (whole * inverse).astype(bf16)
    gram = gram_ref[...]

    def times(x):
        high = x.astype(bf16)
        low = (x - high.astype(f32)).astype(bf16)
        both = jnp.dot(
            jnp.concatenate([high, low], axis=0), gram, preferred_element_type=f32
        )
        return both[:rows] + both[rows:]

    def apply_first(x):
        once = times(x)
        return QUINTIC[0] * x + QUINTIC[1] * once + QUINTIC[2] * times(once)

    def apply_second(x):
        return apply_first(times(apply_first(x)))

    start = velocity_ref[...] / jnp.sqrt(square_sum)
    first = apply_first(start)
    once_more = apply_second(first)
    twice_more = apply_second(once_more)
    final = QUINTIC[0] * first + QUINTIC[1] * once_more + QUINTIC[2] * twice_more
    out_ref[...] = final * jnp.sqrt(jnp.float32(D))


def after(x, earlier):
    return lax.optimization_barrier((x, earlier))[0]


def reduce_over_ring(up, down, middle, ring):
    f32, bf16 = jnp.float32, jnp.bfloat16
    up = shifted(up, -1, ring)
    down = shifted(down, 1, ring)
    sums = {}
    for n, a in enumerate(STEPS):
        sums[a] = middle[n] + down[n].astype(f32)
        if a in UP:
            sums[a] = sums[a] + up[n].astype(f32)
    sums = lax.optimization_barrier(sums)
    got = {}
    last = None
    for k in range(REACH, 0, -1):
        for side in (1, -1):
            total = sums[side * k]
            if side in got:
                total = total + after(got[side], last).astype(f32)
            last = total.astype(bf16) if k in NARROW else total
            got[side] = shifted(last, -side * STRIDE, ring)
    return sums[0] + got[1] + got[-1]


def gram_of(blocks):
    flat = blocks.reshape(-1, blocks.shape[-1])
    return lax.dot_general(
        flat, flat, (((0,), (0,)), ((), ())), preferred_element_type=jnp.float32
    )


def gram_over_ring(own, ring):
    base = jnp.stack([own, shifted(own, -3 * STRIDE, ring), shifted(own, 3 * STRIDE, ring)])
    above = shifted(base, -STRIDE, ring)
    below = shifted(base, STRIDE, ring)
    up = shifted(above[1:2], -STRIDE, ring)
    down = shifted(below[2:3], STRIDE, ring)
    rows = lax.optimization_barrier(jnp.concatenate([base, above, below, down, up]))
    up = shifted(rows[:-1], -1, ring)
    down = shifted(rows, 1, ring)
    return gram_of(rows) + gram_of(up) + gram_of(down)


def local(out_grad, expert_ids, route_gates, hidden_saved, momentum):
    f32, bf16 = jnp.float32, jnp.bfloat16
    n_expert = lax.axis_size("expert")
    ring = lax.axis_size("z")
    z = lax.axis_index("z")
    core = lax.axis_index("core")
    _, d_local, units = momentum.shape
    tok_rows, features = out_grad.shape
    capacity = hidden_saved.shape[3]
    half = features // 2
    own_hidden = hidden_saved.reshape(n_expert, capacity, units)
    other_hidden = swapped(own_hidden)
    outgoing = pl.pallas_call(
        lambda *refs: route_kernel(*refs, experts=n_expert, capacity=capacity),
        out_shape=jax.ShapeDtypeStruct((2 * n_expert, capacity, half), bf16),
        name="route",
    )(expert_ids.reshape(1, tok_rows), route_gates.reshape(1, tok_rows), out_grad)
    received = lax.all_to_all(
        outgoing, ("expert", "core"), split_axis=0, concat_axis=0, tiled=True
    )
    rows = received.reshape(2 * n_expert * capacity, half)
    first_core = core == 0
    hidden = jnp.stack(
        [
            jnp.where(first_core, own_hidden, other_hidden),
            jnp.where(first_core, other_hidden, own_hidden),
        ],
        axis=1,
    ).reshape(2 * n_expert * capacity, units)
    chunk = (z - jnp.array(OFFSETS, dtype=jnp.int32)) % ring
    up, down, middle = pl.pallas_call(
        partial_kernel,
        out_shape=(
            jax.ShapeDtypeStruct((len(UP), d_local, units), bf16),
            jax.ShapeDtypeStruct((len(DOWN), d_local, units), bf16),
            jax.ShapeDtypeStruct((len(STEPS), d_local, units), f32),
        ),
        in_specs=[
            pl.BlockSpec(memory_space=pltpu.SMEM),
            pl.BlockSpec(memory_space=pltpu.VMEM),
            pl.BlockSpec(memory_space=pltpu.VMEM),
        ],
        out_specs=(
            pl.BlockSpec(memory_space=pltpu.VMEM),
            pl.BlockSpec(memory_space=pltpu.VMEM),
            pl.BlockSpec(memory_space=pltpu.VMEM),
        ),
        scratch_shapes=[pltpu.VMEM((ring, d_local, units), f32)],
        name="partial",
    )(chunk, rows, hidden)
    gradient = reduce_over_ring(up, down, middle, ring)
    moment_new = DECAY * momentum[0] + gradient
    velocity = gradient + DECAY * moment_new
    gram = gram_over_ring(velocity.astype(bf16), ring).astype(bf16)
    other_gram = swapped(gram)
    update = pl.pallas_call(
        newton_kernel,
        out_shape=jax.ShapeDtypeStruct((d_local, units), f32),
        scratch_shapes=[pltpu.VMEM((units, units), bf16)],
        name="newton",
    )(velocity, gram, other_gram)
    return moment_new[None], update[None]


def solution(mesh):
    finer = Mesh(
        mesh.devices.reshape(mesh.shape["expert"], mesh.shape["fsdp"] // 2, 2), EXPERT_FSDP
    )
    placed = (
        P(EXPERT_FSDP, None),
        P(EXPERT_FSDP, None),
        P(EXPERT_FSDP, None),
        P("expert", FSDP, None, None, None),
        P("expert", FSDP, None),
    )
    return jax.shard_map(
        local,
        mesh=finer,
        in_specs=placed,
        out_specs=(P("expert", FSDP, None), P("expert", FSDP, None)),
        check_vma=False,
    )
```

```python
import jax
import jax.numpy as jnp
from jax import lax
from jax.experimental import pallas as pl
from jax.experimental.pallas import tpu as pltpu
from jax.sharding import Mesh
from jax.sharding import PartitionSpec as P

D = 2048
FSDP = ("z", "core")
EXPERT_FSDP = ("expert", "z", "core")

QUINTIC = (3.4445, -4.775, 2.0315)
DECAY = 0.95
EPSILON = 1e-07

STRIDE = 3
BASE = (0, 3, -3)
ABOVE = (1, 4, -2)
BELOW = (-1, 2, -4)
STEPS = BASE + ABOVE + BELOW + (-5, 5)
UP = STEPS[:-1]
DOWN = STEPS
OFFSETS = (
    tuple(STRIDE * a + 1 for a in UP)
    + tuple(STRIDE * a - 1 for a in DOWN)
    + tuple(STRIDE * a for a in STEPS)
)


def shifted(x, by, ring):
    return lax.ppermute(x, "z", [(i, (i + by) % ring) for i in range(ring)])


def swapped(x):
    return lax.ppermute(x, "core", [(0, 1), (1, 0)])


def route_kernel(ids_ref, gates_ref, grad_ref, out_ref, *, experts, capacity):
    rows, features = grad_ref.shape
    slots = experts * capacity
    f32, bf16 = jnp.float32, jnp.bfloat16
    ids = ids_ref[...]
    one_hot = lax.broadcasted_iota(jnp.int32, (experts, rows), 0) == ids
    one_hot = jnp.where(one_hot, 1.0, 0.0).astype(f32)
    r = lax.broadcasted_iota(jnp.int32, (rows, rows), 0)
    c = lax.broadcasted_iota(jnp.int32, (rows, rows), 1)
    earlier = jnp.where(r < c, 1.0, 0.0).astype(bf16)
    rank = jnp.dot(one_hot.astype(bf16), earlier, preferred_element_type=f32)
    slot = jnp.sum(rank * one_hot, axis=0, keepdims=True)
    target = ids.astype(f32) * float(capacity) + slot
    place = lax.broadcasted_iota(jnp.int32, (slots, rows), 0).astype(f32)
    placing = jnp.where(place == target, 1.0, 0.0).astype(bf16)
    gates = jnp.transpose(jnp.broadcast_to(gates_ref[...], (128, rows)))[:, 0:1]
    routed = (gates * grad_ref[...].astype(f32)).astype(bf16)
    src = lax.broadcasted_iota(jnp.int32, (256, 256), 0)
    dst = lax.broadcasted_iota(jnp.int32, (256, 256), 1)
    wanted = (dst % 128 // 32) * 64 + (dst // 128) * 32 + dst % 32
    sorting = jnp.where(src == wanted, 1.0, 0.0).astype(bf16)
    for block in range(features // 256):
        columns = routed[:, block * 256 : (block + 1) * 256]
        columns = jnp.dot(columns, sorting, preferred_element_type=f32).astype(bf16)
        placed = jnp.dot(placing, columns, preferred_element_type=f32)
        for e in range(experts):
            piece = placed[e * capacity : (e + 1) * capacity].astype(bf16)
            for core in range(2):
                out_ref[2 * e + core, :, block * 128 : (block + 1) * 128] = piece[
                    :, core * 128 : (core + 1) * 128
                ]


def partial_kernel(chunk_ref, rows_ref, hidden_ref, up_ref, down_ref, middle_ref, part_ref):
    _, size, _ = part_ref.shape
    hidden = hidden_ref[...]
    for block in range(rows_ref.shape[1] // 256):
        part = lax.dot_general(
            rows_ref[:, block * 256 : (block + 1) * 256],
            hidden,
            (((0,), (0,)), ((), ())),
            preferred_element_type=jnp.float32,
        )
        for k in range(256 // size):
            part_ref[block * (256 // size) + k] = part[k * size : (k + 1) * size]
    at = 0
    for ref in (up_ref, down_ref, middle_ref):
        for i in range(ref.shape[0]):
            ref[i] = part_ref[chunk_ref[at]].astype(ref.dtype)
            at += 1


def newton_kernel(velocity_ref, own_ref, other_ref, out_ref, gram_ref):
    f32, bf16 = jnp.float32, jnp.bfloat16
    units = own_ref.shape[0]
    rows = velocity_ref.shape[0]
    trace = jnp.zeros((1, 128), f32)
    eye = lax.broadcasted_iota(jnp.int32, (128, 128), 0) == lax.broadcasted_iota(
        jnp.int32, (128, 128), 1
    )
    for i in range(units // 128):
        at = slice(i * 128, (i + 1) * 128)
        tile = own_ref[at, at].astype(f32) + other_ref[at, at].astype(f32)
        trace = trace + jnp.sum(jnp.where(eye, tile, 0.0), axis=0, keepdims=True)
    square_sum = jnp.sum(trace, axis=1, keepdims=True) + EPSILON
    inverse = 1.0 / square_sum
    whole = own_ref[...].astype(f32) + other_ref[...].astype(f32)
    gram_ref[...] = (whole * inverse).astype(bf16)
    gram = gram_ref[...]

    def times(x):
        high = x.astype(bf16)
        low = (x - high.astype(f32)).astype(bf16)
        both = jnp.dot(
            jnp.concatenate([high, low], axis=0), gram, preferred_element_type=f32
        )
        return both[:rows] + both[rows:]

    def apply_first(x):
        once = times(x)
        return QUINTIC[0] * x + QUINTIC[1] * once + QUINTIC[2] * times(once)

    def apply_second(x):
        return apply_first(times(apply_first(x)))

    start = velocity_ref[...] / jnp.sqrt(square_sum)
    first = apply_first(start)
    once_more = apply_second(first)
    twice_more = apply_second(once_more)
    final = QUINTIC[0] * first + QUINTIC[1] * once_more + QUINTIC[2] * twice_more
    out_ref[...] = final * jnp.sqrt(jnp.float32(D))


def reduce_over_ring(up, down, middle, ring):
    f32, bf16 = jnp.float32, jnp.bfloat16
    up = shifted(up, -1, ring)
    down = shifted(down, 1, ring)
    sums = middle + down.astype(f32)
    sums = jnp.concatenate([sums[:-1] + up.astype(f32), sums[-1:]])
    sums = lax.optimization_barrier(sums)
    base = sums[0:3]
    narrow = lax.optimization_barrier(sums[3:].astype(bf16))
    up = shifted(narrow[0:3], -STRIDE, ring)
    down = shifted(narrow[3:6], STRIDE, ring)
    up_twice = shifted(narrow[7], -2 * STRIDE, ring).astype(f32)
    down_twice = shifted(narrow[6], 2 * STRIDE, ring).astype(f32)
    base = base + up.astype(f32) + down.astype(f32)
    base = jnp.stack([base[0], base[1] + up_twice, base[2] + down_twice])
    far = lax.optimization_barrier((base[0], base[1].astype(bf16), base[2].astype(bf16)))
    up = shifted(far[1], -3 * STRIDE, ring)
    down = shifted(far[2], 3 * STRIDE, ring)
    return far[0] + up.astype(f32) + down.astype(f32)


def gram_of(blocks):
    flat = blocks.reshape(-1, blocks.shape[-1])
    return lax.dot_general(
        flat, flat, (((0,), (0,)), ((), ())), preferred_element_type=jnp.float32
    )


def gram_over_ring(own, ring):
    base = jnp.stack([own, shifted(own, -3 * STRIDE, ring), shifted(own, 3 * STRIDE, ring)])
    above = shifted(base, -STRIDE, ring)
    below = shifted(base, STRIDE, ring)
    up = shifted(base[1:2], -2 * STRIDE, ring)
    down = shifted(base[2:3], 2 * STRIDE, ring)
    rows = lax.optimization_barrier(jnp.concatenate([base, above, below, down, up]))
    up = shifted(rows[:-1], -1, ring)
    down = shifted(rows, 1, ring)
    return gram_of(rows) + gram_of(up) + gram_of(down)


def local(out_grad, expert_ids, route_gates, hidden_saved, momentum):
    f32, bf16 = jnp.float32, jnp.bfloat16
    n_expert = lax.axis_size("expert")
    ring = lax.axis_size("z")
    z = lax.axis_index("z")
    core = lax.axis_index("core")
    _, d_local, units = momentum.shape
    tok_rows, features = out_grad.shape
    capacity = hidden_saved.shape[3]
    half = features // 2
    own_hidden = hidden_saved.reshape(n_expert, capacity, units)
    other_hidden = swapped(own_hidden)
    outgoing = pl.pallas_call(
        lambda *refs: route_kernel(*refs, experts=n_expert, capacity=capacity),
        out_shape=jax.ShapeDtypeStruct((2 * n_expert, capacity, half), bf16),
        name="route",
    )(expert_ids.reshape(1, tok_rows), route_gates.reshape(1, tok_rows), out_grad)
    received = lax.all_to_all(
        outgoing, ("expert", "core"), split_axis=0, concat_axis=0, tiled=True
    )
    rows = received.reshape(2 * n_expert * capacity, half)
    first_core = core == 0
    hidden = jnp.stack(
        [
            jnp.where(first_core, own_hidden, other_hidden),
            jnp.where(first_core, other_hidden, own_hidden),
        ],
        axis=1,
    ).reshape(2 * n_expert * capacity, units)
    chunk = (z - jnp.array(OFFSETS, dtype=jnp.int32)) % ring
    up, down, middle = pl.pallas_call(
        partial_kernel,
        out_shape=(
            jax.ShapeDtypeStruct((len(UP), d_local, units), bf16),
            jax.ShapeDtypeStruct((len(DOWN), d_local, units), bf16),
            jax.ShapeDtypeStruct((len(STEPS), d_local, units), f32),
        ),
        in_specs=[
            pl.BlockSpec(memory_space=pltpu.SMEM),
            pl.BlockSpec(memory_space=pltpu.VMEM),
            pl.BlockSpec(memory_space=pltpu.VMEM),
        ],
        out_specs=(
            pl.BlockSpec(memory_space=pltpu.VMEM),
            pl.BlockSpec(memory_space=pltpu.VMEM),
            pl.BlockSpec(memory_space=pltpu.VMEM),
        ),
        scratch_shapes=[pltpu.VMEM((ring, d_local, units), f32)],
        name="partial",
    )(chunk, rows, hidden)
    gradient = reduce_over_ring(up, down, middle, ring)
    moment_new = DECAY * momentum[0] + gradient
    velocity = gradient + DECAY * moment_new
    gram = gram_over_ring(velocity.astype(bf16), ring).astype(bf16)
    other_gram = swapped(gram)
    update = pl.pallas_call(
        newton_kernel,
        out_shape=jax.ShapeDtypeStruct((d_local, units), f32),
        scratch_shapes=[pltpu.VMEM((units, units), bf16)],
        name="newton",
    )(velocity, gram, other_gram)
    return moment_new[None], update[None]


def solution(mesh):
    finer = Mesh(
        mesh.devices.reshape(mesh.shape["expert"], mesh.shape["fsdp"] // 2, 2), EXPERT_FSDP
    )
    placed = (
        P(EXPERT_FSDP, None),
        P(EXPERT_FSDP, None),
        P(EXPERT_FSDP, None),
        P("expert", FSDP, None, None, None),
        P("expert", FSDP, None),
    )
    return jax.shard_map(
        local,
        mesh=finer,
        in_specs=placed,
        out_specs=(P("expert", FSDP, None), P("expert", FSDP, None)),
        check_vma=False,
    )
```
